32 devices in a mesh: groups: 1, wide: 8 (over y, x, core), narrow: 4 (over z).
Axes of the slice: x: 2, y: 2, z: 4, core: 2. Of those that a mesh axis runs over, the one named last changes fastest.
Arguments:
- table_cells: bfloat16 [128, 128, 192], P(('groups', 'wide', 'narrow')), may hold values from -12 to 12
- counts: int32 [128], P(('groups', 'wide', 'narrow')), may hold values from 32 to 128, as said below
- train_count: int32 [1], P('groups'), may hold values from 32 to 96
- norm_gain: float32 [3, 192], replicated, may hold values from 0.5 to 1.5
- feature_in: bfloat16 [192, 576], P('narrow'), may hold values from -0.4375 to 0.4375
- feature_out: bfloat16 [192, 192], P('narrow'), may hold values from -0.4375 to 0.4375
- sample_in: bfloat16 [192, 576], P('narrow'), may hold values from -0.4375 to 0.4375
- sample_out: bfloat16 [192, 192], P('narrow'), may hold values from -0.4375 to 0.4375
- hidden_up: bfloat16 [192, 768], P('narrow'), may hold values from -0.4375 to 0.4375
- hidden_down: bfloat16 [768, 192], P('narrow'), may hold values from -0.21875 to 0.21875
Outputs:
- updated_cells: bfloat16 [128, 128, 192], P(('groups', 'wide', 'narrow'))
The draws below stay inside these ranges and needn't reach their ends.
Inputs may be any that keep to these rules, and one draw needn't show every extreme that they name: `counts`: feature j of a row is present when j < its count; some row has all 128 features present. Rows 0 to train_count - 1 are the training rows.
All inputs are finite; a program needn't handle non-finite values.
Results may differ from the reference program's by a relative error of at most 0.0086.
Values may be sent and summed in bfloat16 or wider, within the bound.
A program may use at most 64 MiB of HBM per device.

```python
import jax
import jax.numpy as jnp
from jax import lax

E = 192
HEADS = 6
HIDDEN_UNITS = 768
ROWS = 128
FEATS = 128


def draw_table_cells(key, part):
    values = jax.random.normal(key, (ROWS, FEATS, E), jnp.float32)
    return jnp.clip(values, -12.0, 12.0).astype(jnp.bfloat16)


def draw_counts(key, part):
    drawn = jax.random.randint(jax.random.fold_in(key, 11), (ROWS,), FEATS // 4, FEATS + 1).astype(jnp.int32)
    return drawn.at[0].set(FEATS)


def shard_levels(key, dims, cuts, smallest, top_value):
    factor_of = 1.0
    for dim, blocks in cuts:
        draws = jax.random.uniform(jax.random.fold_in(jax.random.fold_in(key, 6), dim), (blocks,), jnp.float32, smallest / len(cuts), top_value / len(cuts))
        factor_of = factor_of * jnp.repeat(jnp.exp(draws), dims[dim] // blocks).reshape((-1,) + (1,) * (len(dims) - 1 - dim))
    return factor_of


def noise(rng, extent, scale, bound, shards=(), dtype=jnp.bfloat16):
    values = scale * jax.random.normal(rng, extent, jnp.float32)
    if shards:
        values = values * shard_levels(rng, extent, shards, -0.22, 0.18)
    return jnp.clip(values, -bound, bound).astype(dtype)


def setup_inputs(seed: int = 0, part: int = 0) -> dict:
    key_of = jax.random.split(jax.random.key(seed), 11)
    part_keys = jax.random.split(jax.random.fold_in(key_of[10], part), 11)
    table_cells = draw_table_cells(jax.random.fold_in(jax.random.fold_in(key_of[10], part), 71), part)
    counts = draw_counts(jax.random.fold_in(jax.random.fold_in(key_of[10], part), 71), part)
    train_count = jax.random.randint(part_keys[2], (1,), ROWS // 4, 3 * ROWS // 4 + 1).astype(jnp.int32)
    norm_gain = jnp.clip(1.0 + 0.1 * jax.random.normal(key_of[3], (3, E), jnp.float32), 0.5, 1.5)
    feature_in = noise(key_of[4], (E, 3 * E), E ** -0.5, 0.4375, ((0, 4),))
    feature_out = noise(key_of[5], (E, E), E ** -0.5, 0.4375, ((0, 4),))
    sample_in = noise(key_of[6], (E, 3 * E), E ** -0.5, 0.4375, ((0, 4),))
    sample_out = noise(key_of[7], (E, E), E ** -0.5, 0.4375, ((0, 4),))
    hidden_up = noise(key_of[8], (E, HIDDEN_UNITS), E ** -0.5, 0.4375, ((0, 4),))
    hidden_down = noise(key_of[9], (HIDDEN_UNITS, E), HIDDEN_UNITS ** -0.5, 0.21875, ((0, 4),))
    return {"table_cells": table_cells, "counts": counts, "train_count": train_count, "norm_gain": norm_gain, "feature_in": feature_in, "feature_out": feature_out, "sample_in": sample_in, "sample_out": sample_out, "hidden_up": hidden_up, "hidden_down": hidden_down}


epsilon = 1e-05

def normalize(values, gain):
    average = lax.optimization_barrier(jnp.mean(values, axis=-1, keepdims=True))
    centered = values - average
    spread = lax.optimization_barrier(jnp.mean(centered * centered, axis=-1, keepdims=True))
    return centered * lax.rsqrt(spread + epsilon) * gain

def attend(packed, valid, head_count):
    length = packed.shape[0]
    model_width = packed.shape[1] // 3
    head_size = model_width // head_count
    queries = packed[:, :model_width].reshape(length, head_count, head_size).astype(jnp.float32)
    key_part = packed[:, model_width:2 * model_width].reshape(length, head_count, head_size).astype(jnp.float32)
    value_part = packed[:, 2 * model_width:].reshape(length, head_count, head_size).astype(jnp.float32)
    scores = jnp.einsum('qhd,khd->hqk', queries, key_part) * (1.0 / jnp.sqrt(jnp.float32(head_size)))
    scores = jnp.where(valid[None, None, :], scores, jnp.float32(-1e+30))
    maxima = lax.optimization_barrier(jnp.max(scores, axis=-1, keepdims=True))
    exponentials = jnp.where(valid[None, None, :], jnp.exp(scores - maxima), jnp.float32(0.0))
    totals = lax.optimization_barrier(jnp.sum(exponentials, axis=-1, keepdims=True))
    probabilities = (exponentials / totals).astype(jnp.bfloat16)
    context = jnp.einsum('hqk,khd->qhd', probabilities.astype(jnp.float32), value_part)
    return context.reshape(length, model_width).astype(jnp.bfloat16)

def reference(table_cells, counts, train_count, norm_gain, feature_in, feature_out, sample_in, sample_out, hidden_up, hidden_down):
    feature_ids = jnp.arange(FEATS).astype(jnp.int32)
    row_ids = jnp.arange(ROWS).astype(jnp.int32)

    def feature_row(pair):
        row_cells, count = pair
        packed = jnp.dot(row_cells, feature_in, preferred_element_type=jnp.float32).astype(jnp.bfloat16)
        context = attend(packed, feature_ids < count, HEADS)
        update = jnp.dot(context, feature_out, preferred_element_type=jnp.float32)
        return normalize(row_cells.astype(jnp.float32) + update, norm_gain[0]).astype(jnp.bfloat16)
    first = lax.map(feature_row, (table_cells, counts))
    columns = jnp.swapaxes(first, 0, 1)
    valid = row_ids < train_count[0]

    def sample_column(column):
        packed = jnp.dot(column, sample_in, preferred_element_type=jnp.float32).astype(jnp.bfloat16)
        context = attend(packed, valid, HEADS)
        update = jnp.dot(context, sample_out, preferred_element_type=jnp.float32)
        second = normalize(column.astype(jnp.float32) + update, norm_gain[1]).astype(jnp.bfloat16)
        hidden = jax.nn.gelu(jnp.dot(second, hidden_up, preferred_element_type=jnp.float32), approximate=False).astype(jnp.bfloat16)
        back = jnp.dot(hidden, hidden_down, preferred_element_type=jnp.float32)
        return normalize(second.astype(jnp.float32) + back, norm_gain[2]).astype(jnp.bfloat16)
    result = lax.map(sample_column, columns)
    return jnp.swapaxes(result, 0, 1)
```

```python
import functools
import math

import jax
import jax.numpy as jnp
from jax import lax
from jax.experimental import pallas as pl
from jax.experimental.pallas import tpu as pltpu
from jax.sharding import PartitionSpec as P

HEADS = 6
EPSILON = 1e-05
MESH = pl.DeviceIdType.MESH
F32 = jnp.float32
BF16 = jnp.bfloat16


def normalize(values, gain):
    average = jnp.mean(values, axis=-1, keepdims=True)
    centered = values - average
    spread = jnp.mean(centered * centered, axis=-1, keepdims=True)
    return centered * lax.rsqrt(spread + EPSILON) * gain


def matmul(a, b):
    return jnp.dot(a, b, preferred_element_type=F32)


def gathered(ref, half):
    parts, _, rows, columns = ref.shape
    if rows % 16 == 0:
        return ref[:, half].reshape(parts * rows, columns)
    pieces = [ref[i, half].astype(F32) for i in range(parts)]
    return jnp.concatenate(pieces, axis=0).astype(BF16)


def reorder(x, source, chunk=512):
    count = x.shape[0]
    chunk = min(chunk, count)
    pieces = []
    for start in range(0, count, chunk):
        to = lax.broadcasted_iota(jnp.int32, (chunk, 1), 0) + start
        column = lax.broadcasted_iota(jnp.int32, (chunk, count), 1)
        pick = jnp.where(column == source(to), 1.0, 0.0).astype(BF16)
        pieces.append(matmul(pick, x).astype(BF16))
    return pieces[0] if len(pieces) == 1 else jnp.concatenate(pieces, axis=0)


def attend(q, k, v, bias):
    length, width = q.shape
    head_size = width // HEADS
    factor = math.log2(math.e) / math.sqrt(head_size)
    head_of = lax.broadcasted_iota(jnp.int32, (length, width), 1) // head_size
    zero = jnp.zeros_like(k)
    masks = [head_of == h for h in range(HEADS)]
    keys = jnp.concatenate([jnp.where(m, k, zero) for m in masks], axis=0)
    values = jnp.concatenate([jnp.where(m, v, zero) for m in masks], axis=0)
    ones = jnp.concatenate([jnp.where(m, 1.0, 0.0).astype(BF16) for m in masks], axis=0)
    scores = lax.dot_general(q, keys, (((1,), (1,)), ((), ())), preferred_element_type=F32)
    powers = []
    for h in range(HEADS):
        s = scores[:, h * length : (h + 1) * length] * factor + bias
        powers.append(jnp.exp2(s - jnp.max(s, axis=-1, keepdims=True)).astype(BF16))
    weight = jnp.concatenate(powers, axis=1)
    return (matmul(weight, values) / matmul(weight, ones)).astype(BF16)


def attention_block(x, w_ref, qkv_ref, ctx_ref, length, bias_of, gain):
    width = x.shape[1]
    left, right = gathered(w_ref, 0), gathered(w_ref, 1)
    qk = matmul(x, left).astype(BF16)
    qkv_ref[0] = qk[:, :width]
    qkv_ref[1] = qk[:, width:]
    qkv_ref[2] = matmul(x, right[:, :width]).astype(BF16)

    def one(i):
        rows = pl.ds(pl.multiple_of(i * length, length), length)
        ctx_ref[rows, :] = attend(
            qkv_ref[0, rows, :], qkv_ref[1, rows, :], qkv_ref[2, rows, :], bias_of(i)
        )

    count = x.shape[0] // length
    if length <= 128:
        for i in range(count):
            one(i)
    else:
        pl.loop(0, count)(one)
    update = matmul(ctx_ref[...], right[:, width:])
    return normalize(x.astype(F32) + update, gain).astype(BF16)


def kernel(
    sizes,
    counts_ref,
    train_ref,
    cells_ref,
    gain_ref,
    fi_ref,
    fo_ref,
    si_ref,
    so_ref,
    hu_ref,
    hd_ref,
    out_ref,
    wf,
    ws,
    wu,
    wd,
    qkv,
    ctx,
    send1,
    recv1,
    send2,
    recv2,
    sa,
    ra,
    sb,
    rb,
    cell_sems,
):
    wide, narrow = sizes
    total = wide * narrow
    g = lax.axis_index("groups")
    w = lax.axis_index("wide")
    n = lax.axis_index("narrow")
    me = w * narrow + n
    core = lax.rem(w, 2)
    mate = w + 1 - 2 * core
    rows, feats, width = cells_ref.shape
    local = feats // total
    block = rows * local
    all_rows = rows * total
    cells = rows * feats

    def device(d):
        return (g, d // narrow, lax.rem(d, narrow))

    barrier = pltpu.get_barrier_semaphore()

    @pl.loop(1, total)
    def _(step):
        pl.semaphore_signal(
            barrier, inc=1, device_id=device(lax.rem(me + step, total)), device_id_type=MESH
        )

    half = 2 * width
    wf[n, 0] = fi_ref[:, :half]
    wf[n, 1] = jnp.concatenate([fi_ref[:, half:], fo_ref[...]], axis=1)
    ws[n, 0] = si_ref[:, :half]
    ws[n, 1] = jnp.concatenate([si_ref[:, half:], so_ref[...]], axis=1)
    wu[n, 0] = hu_ref[:, :half]
    wu[n, 1] = hu_ref[:, half:]
    down = hd_ref.shape[0] // 2
    wd[n, 0] = hd_ref[:down]
    wd[n, 1] = hd_ref[down:]
    pl.semaphore_wait(barrier, total - 1)

    weights = (wf, ws, wu, wd)

    def along(group, step):
        ref = weights[group]
        return pltpu.make_async_remote_copy(
            src_ref=ref.at[n, core],
            dst_ref=ref.at[n, core],
            send_sem=sa.at[group, step],
            recv_sem=ra.at[group, step],
            device_id=(g, w, lax.rem(n + step, narrow)),
            device_id_type=MESH,
        )

    def across(group, step):
        ref = weights[group]
        owner = lax.rem(n - step + narrow, narrow)
        return pltpu.make_async_remote_copy(
            src_ref=ref.at[owner, core],
            dst_ref=ref.at[owner, core],
            send_sem=sb.at[group, step],
            recv_sem=rb.at[group, step],
            device_id=(g, mate, n),
            device_id_type=MESH,
        )

    steps = range(1, narrow)
    for group in range(4):
        for step in steps:
            along(group, step).start()

    def forward(group):
        for step in steps:
            along(group, step).wait_recv()
            across(group, step).start()

    def arrive(group):
        for step in steps:
            across(group, step).wait_recv()

    def exchange(send, recv, index):
        recv[me] = send[me]

        @pl.loop(1, total)
        def _(step):
            d = lax.rem(me + step, total)
            pltpu.make_async_remote_copy(
                src_ref=send.at[d],
                dst_ref=recv.at[me],
                send_sem=cell_sems.at[index],
                recv_sem=cell_sems.at[index + 1],
                device_id=device(d),
                device_id_type=MESH,
            ).start()

    def exchanged(send, recv, index):
        for ref, sem in ((recv, index + 1), (send, index)):
            whole = ref.at[pl.ds(0, total - 1)]
            pltpu.make_async_copy(whole, whole, cell_sems.at[sem]).wait()

    forward(0)
    arrive(0)
    x = cells_ref[...].reshape(cells, width)
    keys = lax.broadcasted_iota(jnp.int32, (1, feats), 1)

    def row_bias(i):
        return jnp.where(keys < counts_ref[i], 0.0, -1e30)

    first = attention_block(x, wf, qkv, ctx, feats, row_bias, gain_ref[0:1, :])

    def to_send(i):
        d, j, r = i // block, (i % block) // rows, i % rows
        return r * feats + d * local + j

    send1[...] = reorder(first, to_send).reshape(total, block, width)
    exchange(send1, recv1, 0)
    for group in (1, 2, 3):
        forward(group)
    arrive(1)
    exchanged(send1, recv1, 0)

    def to_column(i):
        j, s, r = i // all_rows, (i % all_rows) // rows, i % rows
        return s * block + j * rows + r

    y = reorder(recv1[...].reshape(cells, width), to_column)
    samples = lax.broadcasted_iota(jnp.int32, (1, all_rows), 1)
    sample_bias = jnp.where(samples < train_ref[0], 0.0, -1e30)
    second = attention_block(y, ws, qkv, ctx, all_rows, lambda i: sample_bias, gain_ref[1:2, :])

    arrive(2)
    arrive(3)
    ctx[...] = second
    tile = min(512, cells)
    up = [gathered(wu, c) for c in range(2)]
    parts, _, depth, _ = wd.shape
    hidden_width = up[0].shape[1]

    def feed(i):
        at = pl.ds(pl.multiple_of(i * tile, tile), tile)
        values = ctx[at, :]
        halves = []
        for c in range(2):
            h = matmul(values, up[c])
            halves.append((0.5 * h * (1.0 + lax.erf(h * (2.0**-0.5)))).astype(BF16))
        hidden = jnp.concatenate(halves, axis=1)
        back = matmul(hidden, wd[...].reshape(2 * hidden_width, width))
        ctx[at, :] = normalize(values.astype(F32) + back, gain_ref[2:3, :]).astype(BF16)

    if cells == tile:
        feed(0)
    else:
        pl.loop(0, cells // tile)(feed)

    def to_return(i):
        s, j, r = i // block, (i % block) // rows, i % rows
        return j * all_rows + s * rows + r

    send2[...] = reorder(ctx[...], to_return).reshape(total, block, width)
    exchange(send2, recv2, 2)
    for group in range(4):
        for step in steps:
            along(group, step).wait_send()
            across(group, step).wait_send()
    exchanged(send2, recv2, 2)

    def to_row(i):
        r, d, j = i // feats, (i % feats) // local, i % local
        return d * block + j * rows + r

    out_ref[...] = reorder(recv2[...].reshape(cells, width), to_row).reshape(rows, feats, width)


def body(sizes, cells, counts, train, gain, fi, fo, si, so, hu, hd):
    wide, narrow = sizes
    total = wide * narrow
    rows, feats, width = cells.shape
    block = rows * (feats // total)
    shard = fi.shape[0]
    vmem = pl.BlockSpec(memory_space=pltpu.VMEM)
    smem = pl.BlockSpec(memory_space=pltpu.SMEM)
    blocks = pltpu.VMEM((total, block, width), BF16)
    sems = pltpu.SemaphoreType.DMA((4, narrow))
    weight = pltpu.VMEM((narrow, 2, shard, 2 * width), BF16)
    return pl.pallas_call(
        functools.partial(kernel, sizes),
        out_shape=jax.ShapeDtypeStruct(cells.shape, BF16),
        in_specs=[smem, smem] + [vmem] * 8,
        out_specs=vmem,
        scratch_shapes=[
            weight,
            weight,
            weight,
            pltpu.VMEM((narrow, 2, hd.shape[0] // 2, width), BF16),
            pltpu.VMEM((3, rows * feats, width), BF16),
            pltpu.VMEM((rows * feats, width), BF16),
            blocks,
            blocks,
            blocks,
            blocks,
            sems,
            sems,
            sems,
            sems,
            pltpu.SemaphoreType.DMA((4,)),
        ],
        compiler_params=pltpu.CompilerParams(
            collective_id=0, has_side_effects=True, vmem_limit_bytes=56 << 20
        ),
    )(counts, train, cells, gain, fi, fo, si, so, hu, hd)


def solution(mesh):
    sizes = (mesh.shape["wide"], mesh.shape["narrow"])
    return jax.shard_map(
        functools.partial(body, sizes),
        mesh=mesh,
        in_specs=(
            P(("groups", "wide", "narrow"), None, None),
            P(("groups", "wide", "narrow")),
            P("groups"),
            P(),
            P("narrow", None),
            P("narrow", None),
            P("narrow", None),
            P("narrow", None),
            P("narrow", None),
            P("narrow", None),
        ),
        out_specs=P(("groups", "wide", "narrow"), None, None),
        check_vma=False,
    )
```

```python
import functools
import math

import jax
import jax.numpy as jnp
from jax import lax
from jax.experimental import pallas as pl
from jax.experimental.pallas import tpu as pltpu
from jax.sharding import PartitionSpec as P

HEADS = 6
EPSILON = 1e-05
MESH = pl.DeviceIdType.MESH
F32 = jnp.float32
BF16 = jnp.bfloat16


def normalize(values, gain):
    average = jnp.mean(values, axis=-1, keepdims=True)
    centered = values - average
    spread = jnp.mean(centered * centered, axis=-1, keepdims=True)
    return centered * lax.rsqrt(spread + EPSILON) * gain


def matmul(a, b):
    return jnp.dot(a, b, preferred_element_type=F32)


def gathered(ref, part):
    parts, _, rows, columns = ref.shape
    if rows % 16 == 0:
        return ref[:, part].reshape(parts * rows, columns)
    pieces = [ref[i, part].astype(F32) for i in range(parts)]
    return jnp.concatenate(pieces, axis=0).astype(BF16)


def gathered_down(ref, width):
    pieces = []
    for owner in range(ref.shape[0]):
        for part in (2, 3):
            both = ref[owner, part].astype(F32)
            pieces += [both[:, :width], both[:, width:]]
    return jnp.concatenate(pieces, axis=0).astype(BF16)


def one_hot(count, depth, start, source):
    to = lax.broadcasted_iota(jnp.int32, (count, 1), 0) + start
    column = lax.broadcasted_iota(jnp.int32, (count, depth), 1)
    return jnp.where(column == source(to), 1.0, 0.0).astype(BF16)


def reorder(x, count, source, chunk=512):
    chunk = min(chunk, count)
    pieces = [
        matmul(one_hot(chunk, x.shape[0], start, source), x)
        for start in range(0, count, chunk)
    ]
    return pieces[0] if len(pieces) == 1 else jnp.concatenate(pieces, axis=0)


def attend(q, k, v, bias):
    length, width = q.shape
    head_size = width // HEADS
    factor = math.log2(math.e) / math.sqrt(head_size)
    head_of = lax.broadcasted_iota(jnp.int32, (length, width), 1) // head_size
    zero = jnp.zeros_like(k)
    masks = [head_of == h for h in range(HEADS)]
    keys = jnp.concatenate([jnp.where(m, k, zero) for m in masks], axis=0)
    values = jnp.concatenate([jnp.where(m, v, zero) for m in masks], axis=0)
    ones = jnp.concatenate([jnp.where(m, 1.0, 0.0).astype(BF16) for m in masks], axis=0)
    scores = lax.dot_general(q, keys, (((1,), (1,)), ((), ())), preferred_element_type=F32)
    powers = []
    for h in range(HEADS):
        s = scores[:, h * length : (h + 1) * length] * factor + bias
        powers.append(jnp.exp2(s - jnp.max(s, axis=-1, keepdims=True)).astype(BF16))
    weight = jnp.concatenate(powers, axis=1)
    return (matmul(weight, values) / matmul(weight, ones)).astype(BF16)


def attention_block(x, w_ref, part, qkv_ref, ctx_ref, length, bias_of, gain):
    width = x.shape[1]
    left, right = gathered(w_ref, part), gathered(w_ref, part + 1)
    qk = matmul(x, left).astype(BF16)
    qkv_ref[0] = qk[:, :width]
    qkv_ref[1] = qk[:, width:]
    qkv_ref[2] = matmul(x, right[:, :width]).astype(BF16)

    def one(i):
        rows = pl.ds(pl.multiple_of(i * length, length), length)
        ctx_ref[rows, :] = attend(
            qkv_ref[0, rows, :], qkv_ref[1, rows, :], qkv_ref[2, rows, :], bias_of(i)
        )

    count = x.shape[0] // length
    if length <= 128:
        for i in range(count):
            one(i)
    else:
        pl.loop(0, count)(one)
    update = matmul(ctx_ref[...], right[:, width:])
    return normalize(x.astype(F32) + update, gain).astype(BF16)


def kernel(
    sizes,
    counts_ref,
    train_ref,
    gain_ref,
    cells_hbm,
    fi_hbm,
    fo_hbm,
    si_hbm,
    so_hbm,
    hu_hbm,
    hd_hbm,
    out_ref,
    cells_ref,
    fi_ref,
    fo_ref,
    si_ref,
    so_ref,
    hu_ref,
    hd_ref,
    wa,
    wb,
    qkv,
    ctx,
    send1,
    recv1,
    send2,
    recv2,
    sa,
    ra,
    sx,
    rx,
    sb,
    rb,
    cell_sems,
    load_sems,
):
    wide, narrow = sizes
    total = wide * narrow
    g = lax.axis_index("groups")
    w = lax.axis_index("wide")
    n = lax.axis_index("narrow")
    me = w * narrow + n
    core = lax.rem(w, 2)
    mate = w + 1 - 2 * core
    part = lax.rem(w, 4)
    side = part // 2
    near = w + 2 - 4 * side
    far_part = part + 2 - 4 * side
    rows, feats, width = cells_ref.shape
    local = feats // total
    block = rows * local
    all_rows = rows * total
    cells = rows * feats

    def device(d):
        return (g, d // narrow, lax.rem(d, narrow))

    barrier = pltpu.get_barrier_semaphore()

    @pl.loop(1, total)
    def _(step):
        pl.semaphore_signal(
            barrier, inc=1, device_id=device(lax.rem(me + step, total)), device_id_type=MESH
        )

    loads = [
        pltpu.make_async_copy(src, dst, load_sems.at[i])
        for i, (src, dst) in enumerate(
            (
                (fi_hbm, fi_ref),
                (fo_hbm, fo_ref),
                (si_hbm, si_ref),
                (so_hbm, so_ref),
                (hu_hbm, hu_ref),
                (hd_hbm, hd_ref),
                (cells_hbm, cells_ref),
            )
        )
    ]
    for load in loads:
        load.start()
    half = 2 * width
    shard = fi_ref.shape[0]
    for load in loads[:4]:
        load.wait()
    wa[n, 0] = fi_ref[:, :half]
    wa[n, 1] = jnp.concatenate([fi_ref[:, half:], fo_ref[...]], axis=1)
    wa[n, 2] = si_ref[:, :half]
    wa[n, 3] = jnp.concatenate([si_ref[:, half:], so_ref[...]], axis=1)
    for load in loads[4:]:
        load.wait()
    wb[n, 0] = hu_ref[:, :half]
    wb[n, 1] = hu_ref[:, half:]
    down = hd_ref[...].astype(F32)
    for i in range(2):
        top = down[2 * i * shard : (2 * i + 1) * shard]
        low = down[(2 * i + 1) * shard : (2 * i + 2) * shard]
        wb[n, 2 + i] = jnp.concatenate([top, low], axis=1).astype(BF16)
    pl.semaphore_wait(barrier, total - 1)

    weights = (wa, wb)

    def along(group, step):
        ref = weights[group]
        return pltpu.make_async_remote_copy(
            src_ref=ref.at[n, part],
            dst_ref=ref.at[n, part],
            send_sem=sa.at[group, step],
            recv_sem=ra.at[group, step],
            device_id=(g, w, lax.rem(n + step, narrow)),
            device_id_type=MESH,
        )

    def beside(group, step):
        ref = weights[group]
        owner = lax.rem(n - step + narrow, narrow)
        return pltpu.make_async_remote_copy(
            src_ref=ref.at[owner, part],
            dst_ref=ref.at[owner, part],
            send_sem=sx.at[group, step],
            recv_sem=rx.at[group, step],
            device_id=(g, near, n),
            device_id_type=MESH,
        )

    def across(group, far, step):
        ref = weights[group]
        owner = lax.rem(n - step + narrow, narrow)
        which = far_part if far else part
        return pltpu.make_async_remote_copy(
            src_ref=ref.at[owner, which],
            dst_ref=ref.at[owner, which],
            send_sem=sb.at[group, far, step],
            recv_sem=rb.at[group, far, step],
            device_id=(g, mate, n),
            device_id_type=MESH,
        )

    steps = range(1, narrow)
    for group in range(2):
        for step in steps:
            along(group, step).start()

    def forward(group):
        for step in steps:
            along(group, step).wait_recv()
            beside(group, step).start()
            across(group, 0, step).start()

    def forward_far(group):
        for step in steps:
            beside(group, step).wait_recv()
            across(group, 1, step).start()

    def arrive(group):
        for step in steps:
            across(group, 0, step).wait_recv()
            across(group, 1, step).wait_recv()

    def exchange(send, recv, index):
        recv[me] = send[me]

        @pl.loop(1, total)
        def _(step):
            d = lax.rem(me + step, total)
            pltpu.make_async_remote_copy(
                src_ref=send.at[d],
                dst_ref=recv.at[me],
                send_sem=cell_sems.at[index],
                recv_sem=cell_sems.at[index + 1],
                device_id=device(d),
                device_id_type=MESH,
            ).start()

    def exchanged(send, recv, index):
        for ref, sem in ((recv, index + 1), (send, index)):
            whole = ref.at[pl.ds(0, total - 1)]
            pltpu.make_async_copy(whole, whole, cell_sems.at[sem]).wait()

    def packed(first, second):
        both = jnp.concatenate([first, second], axis=1)
        return both.reshape(total, block // 2, 2 * width).astype(BF16)

    def unpacked(ref):
        both = ref[...].astype(F32).reshape(cells // 2, 2 * width).astype(BF16)
        return both[:, :width], both[:, width:]

    forward(0)
    forward_far(0)
    arrive(0)
    x = cells_ref[...].reshape(cells, width)
    keys = lax.broadcasted_iota(jnp.int32, (1, feats), 1)

    def row_bias(i):
        return jnp.where(keys < counts_ref[i], 0.0, -1e30)

    first = attention_block(x, wa, 0, qkv, ctx, feats, row_bias, gain_ref[0:1, :])

    part_rows = block // 2
    part_cells = cells // 2

    def to_send(i):
        h, k = i // part_cells, i % part_cells
        d, j, r = k // part_rows, (k % part_rows) // rows, k % rows
        return r * feats + d * local + h * (local // 2) + j

    picked = reorder(first, cells, to_send)
    send1[...] = packed(picked[:part_cells], picked[part_cells:])
    exchange(send1, recv1, 0)
    forward(1)
    forward_far(1)
    exchanged(send1, recv1, 0)

    def to_column(i):
        j, s, r = i // all_rows, (i % all_rows) // rows, i % rows
        return s * part_rows + j * rows + r

    y = jnp.concatenate(
        [reorder(v, part_cells, to_column).astype(BF16) for v in unpacked(recv1)], axis=0
    )
    samples = lax.broadcasted_iota(jnp.int32, (1, all_rows), 1)
    sample_bias = jnp.where(samples < train_ref[0], 0.0, -1e30)
    second = attention_block(
        y, wa, 2, qkv, ctx, all_rows, lambda i: sample_bias, gain_ref[1:2, :]
    )

    arrive(1)
    ctx[...] = second
    tile = min(512, cells)
    up = [gathered(wb, c) for c in range(2)]
    low = gathered_down(wb, width)

    def feed(i):
        at = pl.ds(pl.multiple_of(i * tile, tile), tile)
        values = ctx[at, :]
        halves = []
        for c in range(2):
            h = matmul(values, up[c])
            halves.append((0.5 * h * (1.0 + lax.erf(h * (2.0**-0.5)))).astype(BF16))
        back = matmul(jnp.concatenate(halves, axis=1), low)
        ctx[at, :] = normalize(values.astype(F32) + back, gain_ref[2:3, :]).astype(BF16)

    if cells == tile:
        feed(0)
    else:
        pl.loop(0, cells // tile)(feed)

    def to_return(i):
        s, j, r = i // part_rows, (i % part_rows) // rows, i % rows
        return j * all_rows + s * rows + r

    send2[...] = packed(
        reorder(ctx[:part_cells, :], part_cells, to_return),
        reorder(ctx[part_cells:, :], part_cells, to_return),
    )
    exchange(send2, recv2, 2)
    for group in range(2):
        for step in steps:
            along(group, step).wait_send()
            beside(group, step).wait_send()
            across(group, 0, step).wait_send()
            across(group, 1, step).wait_send()
    exchanged(send2, recv2, 2)

    def to_row(i):
        r, d, j = i // feats, (i % feats) // local, i % local
        h = j // (local // 2)
        return h * part_cells + d * part_rows + (j % (local // 2)) * rows + r

    landed = jnp.concatenate(unpacked(recv2), axis=0)
    out_ref[...] = reorder(landed, cells, to_row).astype(BF16).reshape(rows, feats, width)


def body(sizes, cells, counts, train, gain, fi, fo, si, so, hu, hd):
    wide, narrow = sizes
    total = wide * narrow
    rows, feats, width = cells.shape
    block = rows * (feats // total)
    shard = fi.shape[0]
    vmem = pl.BlockSpec(memory_space=pltpu.VMEM)
    smem = pl.BlockSpec(memory_space=pltpu.SMEM)
    blocks = pltpu.VMEM((total, block // 2, 2 * width), BF16)
    sems = pltpu.SemaphoreType.DMA((2, narrow))
    far_sems = pltpu.SemaphoreType.DMA((2, 2, narrow))
    weight = pltpu.VMEM((narrow, 4, shard, 2 * width), BF16)
    return pl.pallas_call(
        functools.partial(kernel, sizes),
        out_shape=jax.ShapeDtypeStruct(cells.shape, BF16),
        in_specs=[smem, smem, vmem] + [pl.BlockSpec(memory_space=pl.ANY)] * 7,
        out_specs=vmem,
        scratch_shapes=[
            *[pltpu.VMEM(a.shape, BF16) for a in (cells, fi, fo, si, so, hu, hd)],
            weight,
            weight,
            pltpu.VMEM((3, rows * feats, width), BF16),
            pltpu.VMEM((rows * feats, width), BF16),
            blocks,
            blocks,
            blocks,
            blocks,
            sems,
            sems,
            sems,
            sems,
            far_sems,
            far_sems,
            pltpu.SemaphoreType.DMA((4,)),
            pltpu.SemaphoreType.DMA((7,)),
        ],
        compiler_params=pltpu.CompilerParams(
            collective_id=0, has_side_effects=True, vmem_limit_bytes=56 << 20
        ),
    )(counts, train, gain, cells, fi, fo, si, so, hu, hd)


def solution(mesh):
    sizes = (mesh.shape["wide"], mesh.shape["narrow"])
    return jax.shard_map(
        functools.partial(body, sizes),
        mesh=mesh,
        in_specs=(
            P(("groups", "wide", "narrow"), None, None),
            P(("groups", "wide", "narrow")),
            P("groups"),
            P(),
            P("narrow", None),
            P("narrow", None),
            P("narrow", None),
            P("narrow", None),
            P("narrow", None),
            P("narrow", None),
        ),
        out_specs=P(("groups", "wide", "narrow"), None, None),
        check_vma=False,
    )
```

```python
import functools
import math

import jax
import jax.numpy as jnp
from jax import lax
from jax.experimental import pallas as pl
from jax.experimental.pallas import tpu as pltpu
from jax.sharding import PartitionSpec as P

HEADS = 6
EPSILON = 1e-05
MESH = pl.DeviceIdType.MESH
F32 = jnp.float32
BF16 = jnp.bfloat16


def normalize(values, gain):
    average = jnp.mean(values, axis=-1, keepdims=True)
    centered = values - average
    spread = jnp.mean(centered * centered, axis=-1, keepdims=True)
    return centered * lax.rsqrt(spread + EPSILON) * gain


def matmul(a, b):
    return jnp.dot(a, b, preferred_element_type=F32)


def gathered(ref, part):
    parts, _, rows, columns = ref.shape
    if rows % 16 == 0:
        return ref[:, part].reshape(parts * rows, columns)
    pieces = [ref[i, part].astype(F32) for i in range(parts)]
    return jnp.concatenate(pieces, axis=0).astype(BF16)


def gathered_down(ref, width):
    pieces = []
    for owner in range(ref.shape[0]):
        for part in (2, 3):
            both = ref[owner, part].astype(F32)
            pieces += [both[:, :width], both[:, width:]]
    return jnp.concatenate(pieces, axis=0).astype(BF16)


def one_hot(count, depth, start, source):
    to = lax.broadcasted_iota(jnp.int32, (count, 1), 0) + start
    column = lax.broadcasted_iota(jnp.int32, (count, depth), 1)
    return jnp.where(column == source(to), 1.0, 0.0).astype(BF16)


def prepare(ref, source, chunk=512):
    count, depth = ref.shape
    chunk = min(chunk, count)
    for start in range(0, count, chunk):
        ref[start : start + chunk, :] = one_hot(chunk, depth, start, source)


def reorder(pick, x, start=0, count=None, chunk=512):
    count = pick.shape[0] if count is None else count
    chunk = min(chunk, count)
    pieces = [
        matmul(pick[at : at + chunk, :], x) for at in range(start, start + count, chunk)
    ]
    return pieces[0] if len(pieces) == 1 else jnp.concatenate(pieces, axis=0)


def attend(q, k, v, bias, ones):
    length, width = q.shape
    head_size = width // HEADS
    factor = math.log2(math.e) / math.sqrt(head_size)
    head_of = lax.broadcasted_iota(jnp.int32, (length, width), 1) // head_size
    zero = jnp.zeros_like(k)
    masks = [head_of == h for h in range(HEADS)]
    keys = jnp.concatenate([jnp.where(m, k, zero) for m in masks], axis=0)
    values = jnp.concatenate([jnp.where(m, v, zero) for m in masks], axis=0)
    scores = lax.dot_general(q, keys, (((1,), (1,)), ((), ())), preferred_element_type=F32)
    powers = []
    for h in range(HEADS):
        s = scores[:, h * length : (h + 1) * length] * factor + bias
        powers.append(jnp.exp2(s - jnp.max(s, axis=-1, keepdims=True)).astype(BF16))
    weight = jnp.concatenate(powers, axis=1)
    return (matmul(weight, values) / matmul(weight, ones)).astype(BF16)


def head_ones(ref, length):
    row = lax.broadcasted_iota(jnp.int32, ref.shape, 0) // length
    lane = lax.broadcasted_iota(jnp.int32, ref.shape, 1) // (ref.shape[1] // HEADS)
    ref[...] = jnp.where(row == lane, 1.0, 0.0).astype(BF16)


def attention_block(x, w_ref, part, qkv_ref, ctx_ref, ones_ref, length, bias_of, gain):
    width = x.shape[1]
    left, right = gathered(w_ref, part), gathered(w_ref, part + 1)
    qk = matmul(x, left).astype(BF16)
    qkv_ref[0] = qk[:, :width]
    qkv_ref[1] = qk[:, width:]
    qkv_ref[2] = matmul(x, right[:, :width]).astype(BF16)

    def one(i):
        rows = pl.ds(pl.multiple_of(i * length, length), length)
        ctx_ref[rows, :] = attend(
            qkv_ref[0, rows, :], qkv_ref[1, rows, :], qkv_ref[2, rows, :], bias_of(i), ones_ref[...]
        )

    count = x.shape[0] // length
    if length <= 128:
        for i in range(count):
            one(i)
    else:
        pl.loop(0, count)(one)
    update = matmul(ctx_ref[...], right[:, width:])
    return normalize(x.astype(F32) + update, gain).astype(BF16)


def kernel(
    sizes,
    counts_ref,
    train_ref,
    gain_ref,
    cells_hbm,
    fi_hbm,
    fo_hbm,
    si_hbm,
    so_hbm,
    hu_hbm,
    hd_hbm,
    out_ref,
    cells_ref,
    x_ref,
    fi_ref,
    fo_ref,
    si_ref,
    so_ref,
    hu_ref,
    hd_ref,
    wf,
    ws,
    wb,
    qkv,
    ctx,
    pick_send,
    pick_column,
    pick_return,
    pick_row,
    feature_ones,
    sample_ones,
    send1,
    recv1,
    send2,
    recv2,
    sa,
    ra,
    sx,
    rx,
    sb,
    rb,
    cell_sems,
    load_sems,
):
    wide, narrow = sizes
    total = wide * narrow
    g = lax.axis_index("groups")
    w = lax.axis_index("wide")
    n = lax.axis_index("narrow")
    me = w * narrow + n
    core = lax.rem(w, 2)
    mate = w + 1 - 2 * core
    part = lax.rem(w, 4)
    side = part // 2
    near = w + 2 - 4 * side
    far_part = part + 2 - 4 * side
    rows, width, feats = cells_ref.shape
    local = feats // total
    block = rows * local
    all_rows = rows * total
    cells = rows * feats

    def device(d):
        return (g, d // narrow, lax.rem(d, narrow))

    barrier = pltpu.get_barrier_semaphore()

    @pl.loop(1, total)
    def _(step):
        pl.semaphore_signal(
            barrier, inc=1, device_id=device(lax.rem(me + step, total)), device_id_type=MESH
        )

    loads = [
        pltpu.make_async_copy(src, dst, load_sems.at[i])
        for i, (src, dst) in enumerate(
            (
                (fi_hbm, fi_ref),
                (fo_hbm, fo_ref),
                (si_hbm, si_ref),
                (so_hbm, so_ref),
                (hu_hbm, hu_ref),
                (hd_hbm, hd_ref),
                (cells_hbm, cells_ref),
            )
        )
    ]
    for load in loads:
        load.start()
    half = 2 * width
    shard = fi_ref.shape[0]
    for load in loads[:4]:
        load.wait()
    wf[n, 0] = fi_ref[:, :half]
    wf[n, 1] = jnp.concatenate([fi_ref[:, half:], fo_ref[...]], axis=1)
    ws[n, 0] = si_ref[:, :half]
    ws[n, 1] = jnp.concatenate([si_ref[:, half:], so_ref[...]], axis=1)
    for load in loads[4:]:
        load.wait()
    wb[n, 0] = hu_ref[:, :half]
    wb[n, 1] = hu_ref[:, half:]
    down = hd_ref[...].astype(F32)
    for i in range(2):
        top = down[2 * i * shard : (2 * i + 1) * shard]
        low = down[(2 * i + 1) * shard : (2 * i + 2) * shard]
        wb[n, 2 + i] = jnp.concatenate([top, low], axis=1).astype(BF16)
    for r in range(rows):
        x_ref[r * feats : (r + 1) * feats, :] = cells_ref[r].astype(F32).T.astype(BF16)
    part_rows = block // 2
    part_cells = cells // 2

    def to_send(i):
        h, k = i // part_cells, i % part_cells
        d, j, r = k // part_rows, (k % part_rows) // rows, k % rows
        return r * feats + d * local + h * (local // 2) + j

    def to_column(i):
        j, s, r = i // all_rows, (i % all_rows) // rows, i % rows
        return s * part_rows + j * rows + r

    def to_return(i):
        s, j, r = i // part_rows, (i % part_rows) // rows, i % rows
        return j * all_rows + s * rows + r

    def to_row(i):
        r, d, j = i // feats, (i % feats) // local, i % local
        h = j // (local // 2)
        return h * part_cells + d * part_rows + (j % (local // 2)) * rows + r

    prepare(pick_send, to_send)
    prepare(pick_column, to_column)
    prepare(pick_return, to_return)
    prepare(pick_row, to_row)
    head_ones(feature_ones, feats)
    head_ones(sample_ones, all_rows)
    pl.semaphore_wait(barrier, total - 1)

    weights = (wf, ws, wb)
    mine = (core, core, part)

    def along(group, step):
        ref = weights[group]
        return pltpu.make_async_remote_copy(
            src_ref=ref.at[n, mine[group]],
            dst_ref=ref.at[n, mine[group]],
            send_sem=sa.at[group, step],
            recv_sem=ra.at[group, step],
            device_id=(g, w, lax.rem(n + step, narrow)),
            device_id_type=MESH,
        )

    def beside(step):
        ref = wb
        owner = lax.rem(n - step + narrow, narrow)
        return pltpu.make_async_remote_copy(
            src_ref=ref.at[owner, part],
            dst_ref=ref.at[owner, part],
            send_sem=sx.at[step],
            recv_sem=rx.at[step],
            device_id=(g, near, n),
            device_id_type=MESH,
        )

    def across(group, far, step):
        ref = weights[group]
        owner = lax.rem(n - step + narrow, narrow)
        which = far_part if far else mine[group]
        return pltpu.make_async_remote_copy(
            src_ref=ref.at[owner, which],
            dst_ref=ref.at[owner, which],
            send_sem=sb.at[group, far, step],
            recv_sem=rb.at[group, far, step],
            device_id=(g, mate, n),
            device_id_type=MESH,
        )

    steps = range(1, narrow)
    for step in steps:
        along(0, step).start()

    def forward(group):
        for step in steps:
            along(group, step).wait_recv()
            if group == 2:
                beside(step).start()
            across(group, 0, step).start()

    def forward_far():
        for step in steps:
            beside(step).wait_recv()
            across(2, 1, step).start()

    def arrive(group):
        for step in steps:
            across(group, 0, step).wait_recv()
            if group == 2:
                across(group, 1, step).wait_recv()

    def exchange(send, recv, index):
        recv[me] = send[me]

        @pl.loop(1, total)
        def _(step):
            d = lax.rem(me + step, total)
            pltpu.make_async_remote_copy(
                src_ref=send.at[d],
                dst_ref=recv.at[me],
                send_sem=cell_sems.at[index],
                recv_sem=cell_sems.at[index + 1],
                device_id=device(d),
                device_id_type=MESH,
            ).start()

    def exchanged(send, recv, index):
        for ref, sem in ((recv, index + 1), (send, index)):
            whole = ref.at[pl.ds(0, total - 1)]
            pltpu.make_async_copy(whole, whole, cell_sems.at[sem]).wait()

    def packed(first, second):
        both = jnp.concatenate([first, second], axis=1)
        return both.reshape(total, block // 2, 2 * width).astype(BF16)

    def unpacked(ref):
        both = ref[...].astype(F32).reshape(cells // 2, 2 * width).astype(BF16)
        return both[:, :width], both[:, width:]

    forward(0)
    for group in (1, 2):
        for step in steps:
            along(group, step).start()
    arrive(0)
    x = x_ref[...]
    keys = lax.broadcasted_iota(jnp.int32, (1, feats), 1)

    def row_bias(i):
        return jnp.where(keys < counts_ref[i], 0.0, -1e30)

    first = attention_block(x, wf, 0, qkv, ctx, feature_ones, feats, row_bias, gain_ref[0:1, :])

    picked = reorder(pick_send, first)
    send1[...] = packed(picked[:part_cells], picked[part_cells:])
    exchange(send1, recv1, 0)
    forward(1)
    forward(2)
    forward_far()
    arrive(1)
    exchanged(send1, recv1, 0)

    y = jnp.concatenate(
        [reorder(pick_column, v).astype(BF16) for v in unpacked(recv1)], axis=0
    )
    samples = lax.broadcasted_iota(jnp.int32, (1, all_rows), 1)
    sample_bias = jnp.where(samples < train_ref[0], 0.0, -1e30)
    second = attention_block(
        y, ws, 0, qkv, ctx, sample_ones, all_rows, lambda i: sample_bias, gain_ref[1:2, :]
    )

    arrive(2)
    ctx[...] = second
    tile = min(512, cells)
    up = [gathered(wb, c) for c in range(2)]
    low = gathered_down(wb, width)

    def feed(i):
        at = pl.ds(pl.multiple_of(i * tile, tile), tile)
        values = ctx[at, :]
        halves = []
        for c in range(2):
            h = matmul(values, up[c])
            halves.append((0.5 * h * (1.0 + lax.erf(h * (2.0**-0.5)))).astype(BF16))
        back = matmul(jnp.concatenate(halves, axis=1), low)
        ctx[at, :] = normalize(values.astype(F32) + back, gain_ref[2:3, :]).astype(BF16)

    if cells == tile:
        feed(0)
    else:
        pl.loop(0, cells // tile)(feed)

    send2[...] = packed(
        reorder(pick_return, ctx[:part_cells, :]),
        reorder(pick_return, ctx[part_cells:, :]),
    )
    exchange(send2, recv2, 2)
    for step in steps:
        for group in range(3):
            along(group, step).wait_send()
            across(group, 0, step).wait_send()
        beside(step).wait_send()
        across(2, 1, step).wait_send()
    exchanged(send2, recv2, 2)

    landed = jnp.concatenate(unpacked(recv2), axis=0)
    for r in range(rows):
        ordered = reorder(pick_row, landed, r * feats, feats)
        out_ref[r] = ordered.T.astype(BF16)


def body(sizes, cells, counts, train, gain, fi, fo, si, so, hu, hd):
    wide, narrow = sizes
    total = wide * narrow
    cells = jnp.swapaxes(cells, 1, 2)
    rows, width, feats = cells.shape
    block = rows * (feats // total)
    shard = fi.shape[0]
    vmem = pl.BlockSpec(memory_space=pltpu.VMEM)
    smem = pl.BlockSpec(memory_space=pltpu.SMEM)
    whole = pltpu.VMEM((rows * feats, rows * feats), BF16)
    half = pltpu.VMEM((rows * feats // 2, rows * feats // 2), BF16)
    blocks = pltpu.VMEM((total, block // 2, 2 * width), BF16)
    sems = pltpu.SemaphoreType.DMA((3, narrow))
    near_sems = pltpu.SemaphoreType.DMA((narrow,))
    far_sems = pltpu.SemaphoreType.DMA((3, 2, narrow))
    weight = pltpu.VMEM((narrow, 2, shard, 2 * width), BF16)
    out = pl.pallas_call(
        functools.partial(kernel, sizes),
        out_shape=jax.ShapeDtypeStruct(cells.shape, BF16),
        in_specs=[smem, smem, vmem] + [pl.BlockSpec(memory_space=pl.ANY)] * 7,
        out_specs=vmem,
        scratch_shapes=[
            pltpu.VMEM(cells.shape, BF16),
            pltpu.VMEM((rows * feats, width), BF16),
            *[pltpu.VMEM(a.shape, BF16) for a in (fi, fo, si, so, hu, hd)],
            weight,
            weight,
            pltpu.VMEM((narrow, 4, shard, 2 * width), BF16),
            pltpu.VMEM((3, rows * feats, width), BF16),
            pltpu.VMEM((rows * feats, width), BF16),
            whole,
            half,
            half,
            whole,
            pltpu.VMEM((HEADS * feats, width), BF16),
            pltpu.VMEM((HEADS * rows * total, width), BF16),
            blocks,
            blocks,
            blocks,
            blocks,
            sems,
            sems,
            near_sems,
            near_sems,
            far_sems,
            far_sems,
            pltpu.SemaphoreType.DMA((4,)),
            pltpu.SemaphoreType.DMA((7,)),
        ],
        compiler_params=pltpu.CompilerParams(
            collective_id=0, has_side_effects=True, vmem_limit_bytes=56 << 20
        ),
    )(counts, train, gain, cells, fi, fo, si, so, hu, hd)
    return jnp.swapaxes(out, 1, 2)


def solution(mesh):
    sizes = (mesh.shape["wide"], mesh.shape["narrow"])
    return jax.shard_map(
        functools.partial(body, sizes),
        mesh=mesh,
        in_specs=(
            P(("groups", "wide", "narrow"), None, None),
            P(("groups", "wide", "narrow")),
            P("groups"),
            P(),
            P("narrow", None),
            P("narrow", None),
            P("narrow", None),
            P("narrow", None),
            P("narrow", None),
            P("narrow", None),
        ),
        out_specs=P(("groups", "wide", "narrow"), None, None),
        check_vma=False,
    )
```

```python
import functools
import math

import jax
import jax.numpy as jnp
from jax import lax
from jax.experimental import pallas as pl
from jax.experimental.pallas import tpu as pltpu
from jax.sharding import PartitionSpec as P

HEADS = 6
EPSILON = 1e-05
MESH = pl.DeviceIdType.MESH
F32 = jnp.float32
BF16 = jnp.bfloat16


def normalize(values, gain):
    average = jnp.mean(values, axis=-1, keepdims=True)
    centered = values - average
    spread = jnp.mean(centered * centered, axis=-1, keepdims=True)
    return centered * lax.rsqrt(spread + EPSILON) * gain


def matmul(a, b):
    return jnp.dot(a, b, preferred_element_type=F32)


def gathered(ref, part):
    parts, _, rows, columns = ref.shape
    if rows % 16 == 0:
        return ref[:, part].reshape(parts * rows, columns)
    pieces = [ref[i, part].astype(F32) for i in range(parts)]
    return jnp.concatenate(pieces, axis=0).astype(BF16)


def gathered_down(ref, width):
    pieces = []
    for owner in range(ref.shape[0]):
        for part in (2, 3):
            both = ref[owner, part].astype(F32)
            pieces += [both[:, :width], both[:, width:]]
    return jnp.concatenate(pieces, axis=0).astype(BF16)


def one_hot(count, depth, start, source):
    to = lax.broadcasted_iota(jnp.int32, (count, 1), 0) + start
    column = lax.broadcasted_iota(jnp.int32, (count, depth), 1)
    return jnp.where(column == source(to), 1.0, 0.0).astype(BF16)


def prepare(ref, source, chunk=512):
    count, depth = ref.shape
    chunk = min(chunk, count)
    for start in range(0, count, chunk):
        ref[start : start + chunk, :] = one_hot(chunk, depth, start, source)


def reorder(pick, x, start=0, count=None, chunk=512):
    count = pick.shape[0] if count is None else count
    chunk = min(chunk, count)
    pieces = [
        matmul(pick[at : at + chunk, :], x) for at in range(start, start + count, chunk)
    ]
    return pieces[0] if len(pieces) == 1 else jnp.concatenate(pieces, axis=0)


def attend(q, k, v, bias, ones):
    length, width = q.shape
    head_size = width // HEADS
    factor = math.log2(math.e) / math.sqrt(head_size)
    head_of = lax.broadcasted_iota(jnp.int32, (length, width), 1) // head_size
    zero = jnp.zeros_like(k)
    masks = [head_of == h for h in range(HEADS)]
    keys = jnp.concatenate([jnp.where(m, k, zero) for m in masks], axis=0)
    values = jnp.concatenate([jnp.where(m, v, zero) for m in masks], axis=0)
    scores = lax.dot_general(q, keys, (((1,), (1,)), ((), ())), preferred_element_type=F32)
    powers = []
    for h in range(HEADS):
        s = scores[:, h * length : (h + 1) * length] * factor + bias
        powers.append(jnp.exp2(s - jnp.max(s, axis=-1, keepdims=True)).astype(BF16))
    weight = jnp.concatenate(powers, axis=1)
    return (matmul(weight, values) / matmul(weight, ones)).astype(BF16)


def head_ones(ref, length):
    row = lax.broadcasted_iota(jnp.int32, ref.shape, 0) // length
    lane = lax.broadcasted_iota(jnp.int32, ref.shape, 1) // (ref.shape[1] // HEADS)
    ref[...] = jnp.where(row == lane, 1.0, 0.0).astype(BF16)


def attention_block(x, w_ref, part, qkv_ref, ctx_ref, ones_ref, length, bias_of, gain):
    width = x.shape[1]
    left, right = gathered(w_ref, part), gathered(w_ref, part + 1)
    qk = matmul(x, left).astype(BF16)
    qkv_ref[0] = qk[:, :width]
    qkv_ref[1] = qk[:, width:]
    qkv_ref[2] = matmul(x, right[:, :width]).astype(BF16)

    def one(i):
        rows = pl.ds(pl.multiple_of(i * length, length), length)
        ctx_ref[rows, :] = attend(
            qkv_ref[0, rows, :], qkv_ref[1, rows, :], qkv_ref[2, rows, :], bias_of(i), ones_ref[...]
        )

    count = x.shape[0] // length
    if length <= 128:
        for i in range(count):
            one(i)
    else:
        pl.loop(0, count)(one)
    update = matmul(ctx_ref[...], right[:, width:])
    return normalize(x.astype(F32) + update, gain).astype(BF16)


def kernel(
    sizes,
    counts_ref,
    train_ref,
    gain_ref,
    cells_hbm,
    fi_hbm,
    fo_hbm,
    si_hbm,
    so_hbm,
    hu_hbm,
    hd_hbm,
    out_ref,
    cells_ref,
    x_ref,
    fi_ref,
    fo_ref,
    si_ref,
    so_ref,
    hu_ref,
    hd_ref,
    wf,
    ws,
    wb,
    qkv,
    ctx,
    pick_send,
    pick_column,
    pick_return,
    pick_row,
    feature_ones,
    sample_ones,
    send1,
    recv1,
    send2,
    recv2,
    sa,
    ra,
    sx,
    rx,
    sb,
    rb,
    cell_sems,
    load_sems,
):
    wide, narrow = sizes
    total = wide * narrow
    g = lax.axis_index("groups")
    w = lax.axis_index("wide")
    n = lax.axis_index("narrow")
    me = w * narrow + n
    core = lax.rem(w, 2)
    mate = w + 1 - 2 * core
    part = lax.rem(w, 4)
    side = part // 2
    near = w + 2 - 4 * side
    far_part = part + 2 - 4 * side
    rows, width, feats = cells_ref.shape
    local = feats // total
    block = rows * local
    all_rows = rows * total
    cells = rows * feats

    def device(d):
        return (g, d // narrow, lax.rem(d, narrow))

    barrier = pltpu.get_barrier_semaphore()

    @pl.loop(1, total)
    def _(step):
        pl.semaphore_signal(
            barrier, inc=1, device_id=device(lax.rem(me + step, total)), device_id_type=MESH
        )

    loads = [
        pltpu.make_async_copy(src, dst, load_sems.at[i])
        for i, (src, dst) in enumerate(
            (
                (fi_hbm, fi_ref),
                (fo_hbm, fo_ref),
                (si_hbm, si_ref),
                (so_hbm, so_ref),
                (hu_hbm, hu_ref),
                (hd_hbm, hd_ref),
                (cells_hbm, cells_ref),
            )
        )
    ]
    for load in loads:
        load.start()
    half = 2 * width
    shard = fi_ref.shape[0]
    for load in loads[:4]:
        load.wait()
    wf[n, 0] = fi_ref[:, :half]
    wf[n, 1] = jnp.concatenate([fi_ref[:, half:], fo_ref[...]], axis=1)
    ws[n, 0] = si_ref[:, :half]
    ws[n, 1] = jnp.concatenate([si_ref[:, half:], so_ref[...]], axis=1)
    for load in loads[4:]:
        load.wait()
    wb[n, 0] = hu_ref[:, :half]
    wb[n, 1] = hu_ref[:, half:]
    down = hd_ref[...].astype(F32)
    for i in range(2):
        top = down[2 * i * shard : (2 * i + 1) * shard]
        low = down[(2 * i + 1) * shard : (2 * i + 2) * shard]
        wb[n, 2 + i] = jnp.concatenate([top, low], axis=1).astype(BF16)
    for r in range(rows):
        x_ref[r * feats : (r + 1) * feats, :] = cells_ref[r].astype(F32).T.astype(BF16)
    part_rows = block // 2
    part_cells = cells // 2

    def to_send(i):
        h, k = i // part_cells, i % part_cells
        d, j, r = k // part_rows, (k % part_rows) // rows, k % rows
        return r * feats + d * local + h * (local // 2) + j

    def to_column(i):
        j, s, r = i // all_rows, (i % all_rows) // rows, i % rows
        return s * part_rows + j * rows + r

    def to_return(i):
        s, j, r = i // part_rows, (i % part_rows) // rows, i % rows
        return j * all_rows + s * rows + r

    def to_row(i):
        r, d, j = i // feats, (i % feats) // local, i % local
        h = j // (local // 2)
        return h * part_cells + d * part_rows + (j % (local // 2)) * rows + r

    prepare(pick_send, to_send)
    prepare(pick_column, to_column)
    prepare(pick_return, to_return)
    prepare(pick_row, to_row)
    head_ones(feature_ones, feats)
    head_ones(sample_ones, all_rows)
    pl.semaphore_wait(barrier, total - 1)

    weights = (wf, ws, wb)
    mine = (core, core, part)

    def along(group, step):
        ref = weights[group]
        return pltpu.make_async_remote_copy(
            src_ref=ref.at[n, mine[group]],
            dst_ref=ref.at[n, mine[group]],
            send_sem=sa.at[group, step],
            recv_sem=ra.at[group, step],
            device_id=(g, w, lax.rem(n + step, narrow)),
            device_id_type=MESH,
        )

    def beside(step):
        ref = wb
        owner = lax.rem(n - step + narrow, narrow)
        return pltpu.make_async_remote_copy(
            src_ref=ref.at[owner, part],
            dst_ref=ref.at[owner, part],
            send_sem=sx.at[step],
            recv_sem=rx.at[step],
            device_id=(g, near, n),
            device_id_type=MESH,
        )

    def across(group, far, step):
        ref = weights[group]
        owner = lax.rem(n - step + narrow, narrow)
        which = far_part if far else mine[group]
        return pltpu.make_async_remote_copy(
            src_ref=ref.at[owner, which],
            dst_ref=ref.at[owner, which],
            send_sem=sb.at[group, far, step],
            recv_sem=rb.at[group, far, step],
            device_id=(g, mate, n),
            device_id_type=MESH,
        )

    steps = range(1, narrow)
    for step in steps:
        along(0, step).start()

    def forward(group):
        for step in steps:
            along(group, step).wait_recv()
            if group == 2:
                beside(step).start()
            across(group, 0, step).start()

    def forward_far():
        for step in steps:
            beside(step).wait_recv()
            across(2, 1, step).start()

    def arrive(group):
        for step in steps:
            across(group, 0, step).wait_recv()
            if group == 2:
                across(group, 1, step).wait_recv()

    def exchange(send, recv, index):
        recv[me] = send[me]

        @pl.loop(1, total, unroll=True)
        def _(step):
            d = lax.rem(me + step, total)
            pltpu.make_async_remote_copy(
                src_ref=send.at[d],
                dst_ref=recv.at[me],
                send_sem=cell_sems.at[index],
                recv_sem=cell_sems.at[index + 1],
                device_id=device(d),
                device_id_type=MESH,
            ).start()

    def exchanged(send, recv, index):
        for ref, sem in ((recv, index + 1), (send, index)):
            whole = ref.at[pl.ds(0, total - 1)]
            pltpu.make_async_copy(whole, whole, cell_sems.at[sem]).wait()

    def packed(first, second):
        both = jnp.concatenate([first, second], axis=1)
        return both.reshape(total, block // 2, 2 * width).astype(BF16)

    def unpacked(ref):
        both = ref[...].astype(F32).reshape(cells // 2, 2 * width).astype(BF16)
        return both[:, :width], both[:, width:]

    forward(0)
    for group in (1, 2):
        for step in steps:
            along(group, step).start()
    arrive(0)
    x = x_ref[...]
    keys = lax.broadcasted_iota(jnp.int32, (1, feats), 1)

    def row_bias(i):
        return jnp.where(keys < counts_ref[i], 0.0, -1e30)

    first = attention_block(x, wf, 0, qkv, ctx, feature_ones, feats, row_bias, gain_ref[0:1, :])

    picked = reorder(pick_send, first)
    send1[...] = packed(picked[:part_cells], picked[part_cells:])
    exchange(send1, recv1, 0)
    forward(1)
    forward(2)
    forward_far()
    arrive(1)
    exchanged(send1, recv1, 0)

    y = jnp.concatenate(
        [reorder(pick_column, v).astype(BF16) for v in unpacked(recv1)], axis=0
    )
    samples = lax.broadcasted_iota(jnp.int32, (1, all_rows), 1)
    sample_bias = jnp.where(samples < train_ref[0], 0.0, -1e30)
    second = attention_block(
        y, ws, 0, qkv, ctx, sample_ones, all_rows, lambda i: sample_bias, gain_ref[1:2, :]
    )

    arrive(2)
    ctx[...] = second
    tile = min(512, cells)
    up = [gathered(wb, c) for c in range(2)]
    low = gathered_down(wb, width)

    def feed(i):
        at = pl.ds(pl.multiple_of(i * tile, tile), tile)
        values = ctx[at, :]
        halves = []
        for c in range(2):
            h = matmul(values, up[c])
            halves.append((0.5 * h * (1.0 + lax.erf(h * (2.0**-0.5)))).astype(BF16))
        back = matmul(jnp.concatenate(halves, axis=1), low)
        ctx[at, :] = normalize(values.astype(F32) + back, gain_ref[2:3, :]).astype(BF16)

    if cells == tile:
        feed(0)
    else:
        pl.loop(0, cells // tile)(feed)

    send2[...] = packed(
        reorder(pick_return, ctx[:part_cells, :]),
        reorder(pick_return, ctx[part_cells:, :]),
    )
    exchange(send2, recv2, 2)
    for step in steps:
        for group in range(3):
            along(group, step).wait_send()
            across(group, 0, step).wait_send()
        beside(step).wait_send()
        across(2, 1, step).wait_send()
    exchanged(send2, recv2, 2)

    landed = jnp.concatenate(unpacked(recv2), axis=0)
    for r in range(rows):
        ordered = reorder(pick_row, landed, r * feats, feats)
        out_ref[r] = ordered.T.astype(BF16)


def body(sizes, cells, counts, train, gain, fi, fo, si, so, hu, hd):
    wide, narrow = sizes
    total = wide * narrow
    cells = jnp.swapaxes(cells, 1, 2)
    rows, width, feats = cells.shape
    block = rows * (feats // total)
    shard = fi.shape[0]
    vmem = pl.BlockSpec(memory_space=pltpu.VMEM)
    smem = pl.BlockSpec(memory_space=pltpu.SMEM)
    whole = pltpu.VMEM((rows * feats, rows * feats), BF16)
    half = pltpu.VMEM((rows * feats // 2, rows * feats // 2), BF16)
    blocks = pltpu.VMEM((total, block // 2, 2 * width), BF16)
    sems = pltpu.SemaphoreType.DMA((3, narrow))
    near_sems = pltpu.SemaphoreType.DMA((narrow,))
    far_sems = pltpu.SemaphoreType.DMA((3, 2, narrow))
    weight = pltpu.VMEM((narrow, 2, shard, 2 * width), BF16)
    out = pl.pallas_call(
        functools.partial(kernel, sizes),
        out_shape=jax.ShapeDtypeStruct(cells.shape, BF16),
        in_specs=[smem, smem, vmem] + [pl.BlockSpec(memory_space=pl.ANY)] * 7,
        out_specs=vmem,
        scratch_shapes=[
            pltpu.VMEM(cells.shape, BF16),
            pltpu.VMEM((rows * feats, width), BF16),
            *[pltpu.VMEM(a.shape, BF16) for a in (fi, fo, si, so, hu, hd)],
            weight,
            weight,
            pltpu.VMEM((narrow, 4, shard, 2 * width), BF16),
            pltpu.VMEM((3, rows * feats, width), BF16),
            pltpu.VMEM((rows * feats, width), BF16),
            whole,
            half,
            half,
            whole,
            pltpu.VMEM((HEADS * feats, width), BF16),
            pltpu.VMEM((HEADS * rows * total, width), BF16),
            blocks,
            blocks,
            blocks,
            blocks,
            sems,
            sems,
            near_sems,
            near_sems,
            far_sems,
            far_sems,
            pltpu.SemaphoreType.DMA((4,)),
            pltpu.SemaphoreType.DMA((7,)),
        ],
        compiler_params=pltpu.CompilerParams(
            collective_id=0, has_side_effects=True, vmem_limit_bytes=56 << 20
        ),
    )(counts, train, gain, cells, fi, fo, si, so, hu, hd)
    return jnp.swapaxes(out, 1, 2)


def solution(mesh):
    sizes = (mesh.shape["wide"], mesh.shape["narrow"])
    return jax.shard_map(
        functools.partial(body, sizes),
        mesh=mesh,
        in_specs=(
            P(("groups", "wide", "narrow"), None, None),
            P(("groups", "wide", "narrow")),
            P("groups"),
            P(),
            P("narrow", None),
            P("narrow", None),
            P("narrow", None),
            P("narrow", None),
            P("narrow", None),
            P("narrow", None),
        ),
        out_specs=P(("groups", "wide", "narrow"), None, None),
        check_vma=False,
    )
```
